32 devices in a mesh: row: 8 (over z, core), col: 4 (over y, x).
Axes of the slice: x: 2, y: 2, z: 4, core: 2. Of those that a mesh axis runs over, the one named last changes fastest.
Arguments:
- iterate: bfloat16 [3584, 18432], P('col', 'row'), may hold values from -5.2 to 5.2
Outputs:
- next_iterate: float32 [3584, 18432], P('col', 'row')
The draws below stay inside these ranges and needn't reach their ends.
All inputs are finite; a program needn't handle non-finite values.
Results may differ from the reference program's by a relative error of at most 0.0032.
Values may be sent and summed in bfloat16 or wider, within the bound.
A program may use at most 128 MiB of HBM per device.

```python
import jax
import jax.numpy as jnp

M = 3584
N = 18432


def draw_iterate(key, part):
    key_base, key_level = jax.random.split(key, 2)
    column_group = jnp.arange(N) * 64 // N
    level = jax.random.uniform(key_level, (64,), jnp.float32)
    column_scale = jnp.power(10.0, level)[column_group]
    base = jax.random.truncated_normal(key_base, -4.0, 4.0, (M, N), jnp.float32)
    return (base * column_scale[None, :] * 0.1276).astype(jnp.bfloat16)


def setup_inputs(seed: int = 0) -> dict:
    key_list = jax.random.split(jax.random.key(seed), 2)
    iterate = draw_iterate(jax.random.fold_in(key_list[1], 71), 0)
    return {"iterate": iterate}


QUINTIC_A = 3.4445
QUINTIC_B = -4.7750
QUINTIC_C = 2.0315


def reference(iterate):
    inverse = 1.0 / N
    raw_gram = jnp.dot(iterate, iterate.T, preferred_element_type=jnp.float32)
    gram = (raw_gram * inverse).astype(jnp.bfloat16)
    square = jnp.dot(gram, gram, preferred_element_type=jnp.float32)
    poly = (QUINTIC_B * gram.astype(jnp.float32) + QUINTIC_C * square).astype(jnp.bfloat16)
    product = jnp.dot(poly, iterate, preferred_element_type=jnp.float32)
    return QUINTIC_A * iterate.astype(jnp.float32) + product
```

```python
import functools

import jax
import jax.numpy as jnp
from jax import lax
from jax.experimental import pallas as pl
from jax.experimental.pallas import tpu as pltpu
from jax.sharding import PartitionSpec as P

N = 18432


QUINTIC_A = 3.4445
QUINTIC_B = -4.775
QUINTIC_C = 2.0315

VMEM_LIMIT = 60 * 2**20
EARLY = 4
ROWS_BY_ROWS = (((1,), (1,)), ((), ()))
COLS_BY_ROWS = (((0,), (0,)), ((), ()))


def general(iterate):
    inverse = 1.0 / N
    column_slab = lax.all_gather(iterate, "col", axis=0, tiled=True)
    gram_total = lax.psum_scatter(
        lax.dot_general(column_slab, iterate, ROWS_BY_ROWS, preferred_element_type=jnp.float32),
        "row",
        scatter_dimension=0,
        tiled=True,
    )
    gram_tile = (gram_total * inverse).astype(jnp.bfloat16)
    row_panel = lax.all_gather(gram_tile, "col", axis=1, tiled=True)
    square = jnp.dot(
        row_panel,
        lax.all_gather(gram_tile, "row", axis=0, tiled=True),
        preferred_element_type=jnp.float32,
    )
    poly_tile = (QUINTIC_B * gram_tile.astype(jnp.float32) + QUINTIC_C * square).astype(
        jnp.bfloat16
    )
    product = lax.dot_general(
        lax.all_gather(poly_tile, "row", axis=0, tiled=True),
        column_slab,
        COLS_BY_ROWS,
        preferred_element_type=jnp.float32,
    )
    return QUINTIC_A * iterate.astype(jnp.float32) + product


def polynomial_kernel(
    depth, inverse, early, x_ref, partial_out, poly_out, far_out, pieces,
    slab, part, paired, outgoing, incoming, own, staging, gram, poly, tile,
    x_send, x_recv, far_send, far_recv, pair_send, pair_recv, sum_send, sum_recv,
    own_sem, first_send, first_recv, second_send, second_recv, third_send, third_recv,
    stage_sem, poly_send, poly_recv, out_sem,
):
    m, n = x_ref.shape
    b = 32 * depth
    phases = m // b
    c, r = lax.axis_index("col"), lax.axis_index("row")
    z, core = r // 2, r % 2
    side = r + 1 - 2 * core
    across = {1: c + 1 - 2 * (c % 2), 2: (c + 2) % 4, 3: 3 - c}

    def there(d):
        return (z + d) % depth

    def origin(d):
        return (z + depth - d) % depth

    def remote(source, target, send, recv, row=r, col=c):
        return pltpu.make_async_remote_copy(
            src_ref=source, dst_ref=target, send_sem=send, recv_sem=recv,
            device_id={"row": row, "col": col}, device_id_type=pl.DeviceIdType.MESH,
        )

    barrier = pltpu.get_barrier_semaphore()
    partners = [(r, across[l]) for l in (1, 2, 3)] + [(side, c)]
    partners += [(2 * there(d) + core, c) for d in range(1, depth)]
    for row, col in partners:
        pl.semaphore_signal(
            barrier, inc=1, device_id={"row": row, "col": col},
            device_id_type=pl.DeviceIdType.MESH,
        )
    pl.semaphore_wait(barrier, len(partners))

    def x_copy(q, l):
        rows = pl.ds(q * b, b)
        return remote(
            x_ref.at[rows], slab.at[l - 1, rows],
            x_send.at[q, l - 1], x_recv.at[q, l - 1], col=across[l],
        )

    def far_copy(l):
        rows = pl.ds((l - 1) * (m // 2), m // 2)
        return remote(
            slab.at[l - 1, rows], far_out.at[rows],
            far_send.at[l - 1], far_recv.at[l - 1], col=across[3 - l],
        )

    def pair_copy(q):
        return remote(
            part.at[q % 2, 1 - core], paired.at[q], pair_send.at[q], pair_recv.at[q], row=side
        )

    def products(q):
        low, high = q * b, m - b - q * b

        def put(t, start, left, right):
            width = right.shape[0]
            total = inverse * lax.dot_general(
                left, right, ROWS_BY_ROWS, preferred_element_type=jnp.float32
            )
            total = total.reshape(depth, 2, 16, width)
            for k in (0, 1):
                part[q % 2, k, :, t, :, start : start + width] = total[:, k]

        put(0, 0, slab[0, low : low + b], x_ref[low:])
        put(0, m - low, slab[0, low : low + b], slab[1, : low + b])
        put(1, 0, slab[1, low : low + b], x_ref[low:])
        put(1, m - low, x_ref[high : high + b], x_ref[high:])
        pair_copy(q).start()

    def sum_copy(q, d):
        return remote(
            outgoing.at[q, there(d)], incoming.at[q, d - 1],
            sum_send.at[q, d - 1], sum_recv.at[q, d - 1], row=2 * there(d) + core,
        )

    def send_sums(q):
        pair_copy(q).wait_recv()
        total = part[q % 2, core] + paired[q]
        paired[q] = total
        outgoing[q] = total.astype(jnp.bfloat16)
        for d in range(1, depth):
            sum_copy(q, d).start()

    def first_copy(q, i, arriving=False):
        if q in early:
            return remote(
                own.at[q], pieces.at[q, i, :, z, core],
                first_send.at[q, i - 1], first_recv.at[q, i - 1], col=across[i],
            )
        return remote(
            own.at[q], pieces.at[q, 0, :, origin(i) if arriving else z, core],
            first_send.at[q, i - 1], first_recv.at[q, i - 1], row=2 * there(i) + core,
        )

    def second_copy(q, i, arriving=False):
        if q in early:
            held = pieces.at[q, :, :, origin(i) if arriving else z, core]
            return remote(
                held, held, second_send.at[q, i - 1], second_recv.at[q, i - 1],
                row=2 * there(i) + core,
            )
        return remote(
            pieces.at[q, 0, :, :, core], pieces.at[q, i, :, :, core],
            second_send.at[q, i - 1], second_recv.at[q, i - 1], col=across[i],
        )

    def third_copy(q, arriving=False):
        held = pieces.at[q, :, :, :, 1 - core if arriving else core]
        return remote(held, held, third_send.at[q], third_recv.at[q], row=side)

    def own_copy(q):
        return pltpu.make_async_copy(own.at[q], pieces.at[q, 0, :, z, core], own_sem.at[q])

    def count(q, second):
        return 3 if (q in early) != second else depth - 1

    def first(q):
        total = paired[q, z]
        for d in range(1, depth):
            sum_copy(q, d).wait_recv()
            total += incoming[q, d - 1].astype(jnp.float32)
        own[q] = total.astype(jnp.bfloat16)
        own_copy(q).start()
        for i in range(1, count(q, False) + 1):
            first_copy(q, i).start()

    def second(q):
        own_copy(q).wait()
        for i in range(1, count(q, False) + 1):
            first_copy(q, i, True).wait_recv()
        for i in range(1, count(q, True) + 1):
            second_copy(q, i).start()

    def third(q):
        for i in range(1, count(q, True) + 1):
            second_copy(q, i, True).wait_recv()
        third_copy(q).start()

    def stage(q):
        return pltpu.make_async_copy(pieces.at[q], staging.at[q % 2], stage_sem.at[q % 2])

    def arrived(q):
        third_copy(q, True).wait_recv()
        stage(q).start()

    def assemble(q):
        stage(q).wait()
        low, high = q * b, m - b - q * b

        def place(block, row, lane_block, lane, value, flipped):
            width = value.shape[1]
            rows, lanes = block * m + row, lane_block * m + lane
            gram[rows : rows + b, lanes : lanes + width] = value
            gram[lanes : lanes + width, rows : rows + b] = flipped

        for l in range(4):
            value = staging[q % 2, l, 0].reshape(b, m + b)
            flipped = value.T
            cut = m - low
            place(l ^ 1, low, l, low, value[:, :cut], flipped[:cut])
            place(l ^ 1, low, l ^ 2, 0, value[:, cut:], flipped[cut:])
            value = staging[q % 2, l, 1].reshape(b, m + b)
            flipped = value.T
            place(l ^ 2, low, l, low, value[:, :cut], flipped[:cut])
            place(l, high, l, high, value[:, cut:], flipped[cut:])

    for q in range(2):
        for l in (1, 2):
            x_copy(q, l).start()
    for q in range(phases):
        for l in (1, 2):
            x_copy(q, l).wait()
        if q + 2 < phases:
            for l in (1, 2):
                x_copy(q + 2, l).start()
        if q > 1:
            pair_copy(q - 2).wait_send()
        products(q)
        if q > 0:
            first(q - 1)
        send_sums(q)
        if q > 1:
            second(q - 2)
        if q > 2:
            third(q - 3)
        if q > 3:
            arrived(q - 4)
            assemble(q - 4)
    last = phases - 1
    first(last)
    second(last - 1)
    second(last)
    for l in (1, 2):
        far_copy(l).start()
    third(last - 2)
    arrived(last - 3)
    assemble(last - 3)
    third(last - 1)
    arrived(last - 2)
    assemble(last - 2)
    third(last)
    arrived(last - 1)
    assemble(last - 1)
    arrived(last)
    assemble(last)

    width = 256
    tiles = 2 * m // width

    def poly_copy(i, half):
        lanes = pl.ds(pl.multiple_of(half * 2 * m + i * width, width), width)
        return remote(poly.at[:, lanes], poly.at[:, lanes], poly_send.at[i], poly_recv.at[i], row=side)

    def square(i, carry):
        lanes = pl.ds(pl.multiple_of(core * 2 * m + i * width, width), width)
        total = jnp.dot(gram[:m], gram[:, lanes], preferred_element_type=jnp.float32)
        kept = gram[:m, lanes].astype(jnp.float32)
        poly[:, lanes] = (QUINTIC_B * kept + QUINTIC_C * total).astype(jnp.bfloat16)
        poly_copy(i, core).start()
        return carry

    lax.fori_loop(0, tiles, square, 0)
    for i in range(tiles):
        poly_copy(i, 1 - core).wait_recv()
    keep = pltpu.make_async_copy(poly.at[:, pl.ds(3 * m, m)], poly_out, out_sem.at[2])
    keep.start()

    def out_copy(i):
        lanes = pl.ds(pl.multiple_of(i * width, width), width)
        return pltpu.make_async_copy(tile.at[i % 2], partial_out.at[:, lanes], out_sem.at[i % 2])

    def product(i, carry):
        lanes = pl.ds(pl.multiple_of(i * width, width), width)
        pl.when(i > 1)(lambda: out_copy(i - 2).wait())
        total = jnp.dot(poly[:, :m], x_ref[:, lanes], preferred_element_type=jnp.float32)
        for l in (1, 2):
            total += jnp.dot(
                poly[:, l * m : (l + 1) * m], slab[l - 1, :, lanes],
                preferred_element_type=jnp.float32,
            )
        tile[i % 2] = total
        out_copy(i).start()
        return carry

    lax.fori_loop(0, n // width, product, 0)
    for i in (n // width - 2, n // width - 1):
        out_copy(i).wait()
    keep.wait()
    for l in (1, 2):
        far_copy(l).wait()
    for i in range(tiles):
        poly_copy(i, core).wait_send()
    for q in range(phases):
        if q > phases - 3:
            pair_copy(q).wait_send()
        for d in range(1, depth):
            sum_copy(q, d).wait_send()
        for i in range(1, count(q, False) + 1):
            first_copy(q, i).wait_send()
        for i in range(1, count(q, True) + 1):
            second_copy(q, i).wait_send()
        third_copy(q).wait_send()


def square_of_four(rows, iterate):
    m, n = iterate.shape
    depth = rows // 2
    b = 16 * rows
    phases, lanes = m // b, m + b
    bf16, f32, dma = jnp.bfloat16, jnp.float32, pltpu.SemaphoreType.DMA
    anywhere = pl.BlockSpec(memory_space=pl.ANY)
    partial, poly, far, _ = pl.pallas_call(
        functools.partial(polynomial_kernel, depth, 1.0 / N, tuple(range(EARLY))),
        out_shape=(
            jax.ShapeDtypeStruct((m, n), f32),
            jax.ShapeDtypeStruct((m, m), bf16),
            jax.ShapeDtypeStruct((m, n), bf16),
            jax.ShapeDtypeStruct((phases, 4, 2, depth, 2, 16, lanes), bf16),
        ),
        in_specs=[pl.BlockSpec(memory_space=pltpu.VMEM)],
        out_specs=(anywhere,) * 4,
        scratch_shapes=[
            pltpu.VMEM((2, m, n), bf16),
            pltpu.VMEM((2, 2, depth, 2, 16, lanes), f32),
            pltpu.VMEM((phases, depth, 2, 16, lanes), f32),
            pltpu.VMEM((phases, depth, 2, 16, lanes), bf16),
            pltpu.VMEM((phases, depth - 1, 2, 16, lanes), bf16),
            pltpu.VMEM((phases, 2, 16, lanes), bf16),
            pltpu.VMEM((2, 4, 2, depth, 2, 16, lanes), bf16),
            pltpu.VMEM((4 * m, 4 * m), bf16),
            pltpu.VMEM((m, 4 * m), bf16),
            pltpu.VMEM((2, m, 256), f32),
            dma((phases, 2)), dma((phases, 2)),
            dma((2,)), dma((2,)),
            dma((phases,)), dma((phases,)),
            dma((phases, depth - 1)), dma((phases, depth - 1)),
            dma((phases,)),
            dma((phases, 3)), dma((phases, 3)),
            dma((phases, 3)), dma((phases, 3)),
            dma((phases,)), dma((phases,)),
            dma((2,)),
            dma((2 * m // 256,)), dma((2 * m // 256,)),
            dma((3,)),
        ],
        compiler_params=pltpu.CompilerParams(
            collective_id=0, has_side_effects=True, vmem_limit_bytes=VMEM_LIMIT
        ),
    )(iterate)
    product = partial + jnp.dot(poly, far, preferred_element_type=f32)
    return QUINTIC_A * iterate.astype(f32) + product


def solution(mesh):
    rows, cols = mesh.shape["row"], mesh.shape["col"]
    placed = (P("col", "row"),)

    def local(iterate):
        m, n = iterate.shape
        fits = 40 * m * m + 6 * m * n + 15000 * m < VMEM_LIMIT
        if cols == 4 and rows == 8 and m % 128 == 0 and m >= 512 and n % 256 == 0 and fits:
            return square_of_four(rows, iterate)
        return general(iterate)

    return jax.shard_map(
        local, mesh=mesh, in_specs=placed, out_specs=P("col", "row"), check_vma=False
    )
```

```python
import functools

import jax
import jax.numpy as jnp
from jax import lax
from jax.experimental import pallas as pl
from jax.experimental.pallas import tpu as pltpu
from jax.sharding import PartitionSpec as P

N = 18432


QUINTIC_A = 3.4445
QUINTIC_B = -4.775
QUINTIC_C = 2.0315

VMEM_LIMIT = 60 * 2**20
EARLY = (0,)
LAG = (4, 5)
FAR_STEP = (9, 9, 9, 9, 9, 9, 9)
ROWS_BY_ROWS = (((1,), (1,)), ((), ()))
COLS_BY_ROWS = (((0,), (0,)), ((), ()))


def general(iterate):
    inverse = 1.0 / N
    column_slab = lax.all_gather(iterate, "col", axis=0, tiled=True)
    gram_total = lax.psum_scatter(
        lax.dot_general(column_slab, iterate, ROWS_BY_ROWS, preferred_element_type=jnp.float32),
        "row",
        scatter_dimension=0,
        tiled=True,
    )
    gram_tile = (gram_total * inverse).astype(jnp.bfloat16)
    row_panel = lax.all_gather(gram_tile, "col", axis=1, tiled=True)
    square = jnp.dot(
        row_panel,
        lax.all_gather(gram_tile, "row", axis=0, tiled=True),
        preferred_element_type=jnp.float32,
    )
    poly_tile = (QUINTIC_B * gram_tile.astype(jnp.float32) + QUINTIC_C * square).astype(
        jnp.bfloat16
    )
    product = lax.dot_general(
        lax.all_gather(poly_tile, "row", axis=0, tiled=True),
        column_slab,
        COLS_BY_ROWS,
        preferred_element_type=jnp.float32,
    )
    return QUINTIC_A * iterate.astype(jnp.float32) + product


def polynomial_kernel(
    depth, inverse, early, x_ref, partial_out, poly_out, far_out, pieces,
    slab, part, paired, outgoing, incoming, own, staging, gram, poly, tile,
    x_send, x_recv, far_send, far_recv, pair_send, pair_recv, sum_send, sum_recv,
    own_sem, along_send, along_recv, plane_send, plane_recv, relay_send, relay_recv,
    third_send, third_recv,
    stage_sem, poly_send, poly_recv, out_sem,
):
    m, n = x_ref.shape
    b = 32 * depth
    phases = m // b
    c, r = lax.axis_index("col"), lax.axis_index("row")
    z, core = r // 2, r % 2
    side = r + 1 - 2 * core
    across = {1: c + 1 - 2 * (c % 2), 2: (c + 2) % 4, 3: 3 - c}

    def there(d):
        return (z + d) % depth

    def origin(d):
        return (z + depth - d) % depth

    def remote(source, target, send, recv, row=r, col=c):
        return pltpu.make_async_remote_copy(
            src_ref=source, dst_ref=target, send_sem=send, recv_sem=recv,
            device_id={"row": row, "col": col}, device_id_type=pl.DeviceIdType.MESH,
        )

    barrier = pltpu.get_barrier_semaphore()
    partners = [(r, across[l]) for l in (1, 2, 3)] + [(side, c)]
    partners += [(2 * there(d) + core, c) for d in range(1, depth)]
    for row, col in partners:
        pl.semaphore_signal(
            barrier, inc=1, device_id={"row": row, "col": col},
            device_id_type=pl.DeviceIdType.MESH,
        )
    pl.semaphore_wait(barrier, len(partners))

    def x_copy(q, l):
        rows = pl.ds(q * b, b)
        return remote(
            x_ref.at[rows], slab.at[l - 1, rows],
            x_send.at[q, l - 1], x_recv.at[q, l - 1], col=across[l],
        )

    def far_copy(q, l):
        rows = pl.ds(q * b + (l - 1) * (b // 2), b // 2)
        return remote(
            slab.at[l - 1, rows], far_out.at[rows],
            far_send.at[q, l - 1], far_recv.at[q, l - 1], col=across[3 - l],
        )

    def pair_copy(q):
        return remote(
            part.at[q % 2, 1 - core], paired.at[q], pair_send.at[q], pair_recv.at[q], row=side
        )

    def products(q):
        low, high = q * b, m - b - q * b

        def put(t, start, left, right):
            width = right.shape[0]
            total = inverse * lax.dot_general(
                left, right, ROWS_BY_ROWS, preferred_element_type=jnp.float32
            )
            total = total.reshape(depth, 2, 16, width)
            for k in (0, 1):
                part[q % 2, k, :, t, :, start : start + width] = total[:, k]

        put(0, 0, slab[0, low : low + b], x_ref[low:])
        put(0, m - low, slab[0, low : low + b], slab[1, : low + b])
        put(1, 0, slab[1, low : low + b], x_ref[low:])
        put(1, m - low, x_ref[high : high + b], x_ref[high:])
        pair_copy(q).start()

    def sum_copy(q, d):
        return remote(
            outgoing.at[q, there(d)], incoming.at[q, d - 1],
            sum_send.at[q, d - 1], sum_recv.at[q, d - 1], row=2 * there(d) + core,
        )

    def send_sums(q):
        pair_copy(q).wait_recv()
        total = part[q % 2, core] + paired[q]
        paired[q] = total
        outgoing[q] = total.astype(jnp.bfloat16)
        for d in range(1, depth):
            sum_copy(q, d).start()

    def along_copy(q, d, arriving=False):
        at = origin(d) if arriving else z
        held = pieces.at[q, :, :, at, core] if q in early else pieces.at[q, 0, :, at, core]
        return remote(
            held if q in early else own.at[q], held,
            along_send.at[q, d - 1], along_recv.at[q, d - 1], row=2 * there(d) + core,
        )

    def plane_copy(q, l):
        if q in early:
            source, held = own.at[q], pieces.at[q, l, :, z, core]
        else:
            source, held = pieces.at[q, 0, :, :, core], pieces.at[q, l, :, :, core]
        return remote(
            source, held, plane_send.at[q, l - 1], plane_recv.at[q, l - 1], col=across[l]
        )

    def relay_copy(q, l):
        if q in early:
            source, held = pieces.at[q, l, l - 1, z, core], pieces.at[q, 3, l - 1, z, core]
        else:
            source, held = pieces.at[q, l, l - 1, :, core], pieces.at[q, 3, l - 1, :, core]
        return remote(
            source, held, relay_send.at[q, l - 1], relay_recv.at[q, l - 1], col=across[3 - l]
        )

    def third_copy(q, arriving=False):
        held = pieces.at[q, :, :, :, 1 - core if arriving else core]
        return remote(held, held, third_send.at[q], third_recv.at[q], row=side)

    def own_copy(q):
        return pltpu.make_async_copy(own.at[q], pieces.at[q, 0, :, z, core], own_sem.at[q])

    def finish(q):
        total = paired[q, z]
        for d in range(1, depth):
            sum_copy(q, d).wait_recv()
            total += incoming[q, d - 1].astype(jnp.float32)
        own[q] = total.astype(jnp.bfloat16)
        own_copy(q).start()

    def start_along(q):
        for d in range(1, depth):
            along_copy(q, d).start()

    def along_arrived(q):
        for d in range(1, depth):
            along_copy(q, d, True).wait_recv()

    def start_plane(q):
        for l in (1, 2):
            plane_copy(q, l).start()

    def start_relay(q):
        for l in (1, 2):
            plane_copy(q, l).wait_recv()
        for l in (1, 2):
            relay_copy(q, l).start()

    def relay_arrived(q):
        for l in (1, 2):
            relay_copy(q, l).wait_recv()

    def first(q):
        finish(q)
        if q in early:
            start_plane(q)
        else:
            start_along(q)

    def second(q):
        own_copy(q).wait()
        if q in early:
            start_relay(q)
        else:
            along_arrived(q)
            start_plane(q)

    def third(q):
        if q in early:
            relay_arrived(q)
            start_along(q)
        else:
            start_relay(q)

    def fourth(q):
        if q in early:
            along_arrived(q)
        else:
            relay_arrived(q)
        third_copy(q).start()

    def stage(q):
        return pltpu.make_async_copy(pieces.at[q], staging.at[q % 2], stage_sem.at[q])

    def arrived(q):
        third_copy(q, True).wait_recv()
        stage(q).start()

    def assemble(q):
        stage(q).wait()
        low, high = q * b, m - b - q * b

        def place(block, row, lane_block, lane, value, flipped):
            width = value.shape[1]
            rows, lanes = block * m + row, lane_block * m + lane
            gram[rows : rows + b, lanes : lanes + width] = value
            gram[lanes : lanes + width, rows : rows + b] = flipped

        for l in range(4):
            value = staging[q % 2, l, 0].reshape(b, m + b)
            flipped = value.T
            cut = m - low
            place(l ^ 1, low, l, low, value[:, :cut], flipped[:cut])
            place(l ^ 1, low, l ^ 2, 0, value[:, cut:], flipped[cut:])
            value = staging[q % 2, l, 1].reshape(b, m + b)
            flipped = value.T
            place(l ^ 2, low, l, low, value[:, :cut], flipped[:cut])
            place(l, high, l, high, value[:, cut:], flipped[cut:])

    for q in range(2):
        for l in (1, 2):
            x_copy(q, l).start()
    stages = (
        (first, (1, 1)), (second, (2, 2)), (third, (3, 3)), (fourth, LAG), (arrived, (LAG[0] + 1, LAG[1] + 1))
    )
    for step in range(phases + max(LAG) + 1):
        if step < phases:
            for l in (1, 2):
                x_copy(step, l).wait()
            if step + 2 < phases:
                for l in (1, 2):
                    x_copy(step + 2, l).start()
            if step > 1:
                pair_copy(step - 2).wait_send()
            products(step)
        for act, lags in stages:
            for q in range(phases):
                if q + lags[q in early] == step:
                    act(q)
            if act is first and step < phases:
                send_sums(step)
        for q in range(phases):
            if FAR_STEP[q] == step:
                for l in (1, 2):
                    far_copy(q, l).start()
        for q in range(phases):
            if q + LAG[q in early] + 1 == step:
                assemble(q)

    width = 256
    tiles = 2 * m // width

    def poly_copy(i, half):
        lanes = pl.ds(pl.multiple_of(half * 2 * m + i * width, width), width)
        return remote(poly.at[:, lanes], poly.at[:, lanes], poly_send.at[i], poly_recv.at[i], row=side)

    def square(i, carry):
        lanes = pl.ds(pl.multiple_of(core * 2 * m + i * width, width), width)
        total = jnp.dot(gram[:m], gram[:, lanes], preferred_element_type=jnp.float32)
        kept = gram[:m, lanes].astype(jnp.float32)
        poly[:, lanes] = (QUINTIC_B * kept + QUINTIC_C * total).astype(jnp.bfloat16)
        poly_copy(i, core).start()
        return carry

    lax.fori_loop(0, tiles, square, 0)
    for i in range(tiles):
        poly_copy(i, 1 - core).wait_recv()
    keep = pltpu.make_async_copy(poly.at[:, pl.ds(3 * m, m)], poly_out, out_sem.at[2])
    keep.start()

    def out_copy(i):
        lanes = pl.ds(pl.multiple_of(i * width, width), width)
        return pltpu.make_async_copy(tile.at[i % 2], partial_out.at[:, lanes], out_sem.at[i % 2])

    def product(i, carry):
        lanes = pl.ds(pl.multiple_of(i * width, width), width)
        pl.when(i > 1)(lambda: out_copy(i - 2).wait())
        total = QUINTIC_A * x_ref[:, lanes].astype(jnp.float32)
        total += jnp.dot(poly[:, :m], x_ref[:, lanes], preferred_element_type=jnp.float32)
        for l in (1, 2):
            total += jnp.dot(
                poly[:, l * m : (l + 1) * m], slab[l - 1, :, lanes],
                preferred_element_type=jnp.float32,
            )
        tile[i % 2] = total
        out_copy(i).start()
        return carry

    lax.fori_loop(0, n // width, product, 0)
    for i in (n // width - 2, n // width - 1):
        out_copy(i).wait()
    keep.wait()
    for q in range(phases):
        for l in (1, 2):
            far_copy(q, l).wait()
    for i in range(tiles):
        poly_copy(i, core).wait_send()
    for q in range(phases):
        if q > phases - 3:
            pair_copy(q).wait_send()
        for d in range(1, depth):
            sum_copy(q, d).wait_send()
        for d in range(1, depth):
            along_copy(q, d).wait_send()
        for l in (1, 2):
            plane_copy(q, l).wait_send()
            relay_copy(q, l).wait_send()
        third_copy(q).wait_send()


def last_product(partial_ref, poly_ref, far_ref, out_ref):
    out_ref[...] = partial_ref[...] + jnp.dot(
        poly_ref[...], far_ref[...], preferred_element_type=jnp.float32
    )


def square_of_four(rows, iterate):
    m, n = iterate.shape
    depth = rows // 2
    b = 16 * rows
    phases, lanes = m // b, m + b
    bf16, f32, dma = jnp.bfloat16, jnp.float32, pltpu.SemaphoreType.DMA
    anywhere = pl.BlockSpec(memory_space=pl.ANY)
    partial, poly, far, _ = pl.pallas_call(
        functools.partial(polynomial_kernel, depth, 1.0 / N, EARLY),
        out_shape=(
            jax.ShapeDtypeStruct((m, n), f32),
            jax.ShapeDtypeStruct((m, m), bf16),
            jax.ShapeDtypeStruct((m, n), bf16),
            jax.ShapeDtypeStruct((phases, 4, 2, depth, 2, 16, lanes), bf16),
        ),
        in_specs=[pl.BlockSpec(memory_space=pltpu.VMEM)],
        out_specs=(anywhere,) * 4,
        scratch_shapes=[
            pltpu.VMEM((2, m, n), bf16),
            pltpu.VMEM((2, 2, depth, 2, 16, lanes), f32),
            pltpu.VMEM((phases, depth, 2, 16, lanes), f32),
            pltpu.VMEM((phases, depth, 2, 16, lanes), bf16),
            pltpu.VMEM((phases, depth - 1, 2, 16, lanes), bf16),
            pltpu.VMEM((phases, 2, 16, lanes), bf16),
            pltpu.VMEM((2, 4, 2, depth, 2, 16, lanes), bf16),
            pltpu.VMEM((4 * m, 4 * m), bf16),
            pltpu.VMEM((m, 4 * m), bf16),
            pltpu.VMEM((2, m, 256), f32),
            dma((phases, 2)), dma((phases, 2)),
            dma((phases, 2)), dma((phases, 2)),
            dma((phases,)), dma((phases,)),
            dma((phases, depth - 1)), dma((phases, depth - 1)),
            dma((phases,)),
            dma((phases, depth - 1)), dma((phases, depth - 1)),
            dma((phases, 2)), dma((phases, 2)),
            dma((phases, 2)), dma((phases, 2)),
            dma((phases,)), dma((phases,)),
            dma((phases,)),
            dma((2 * m // 256,)), dma((2 * m // 256,)),
            dma((3,)),
        ],
        compiler_params=pltpu.CompilerParams(
            collective_id=0, has_side_effects=True, vmem_limit_bytes=VMEM_LIMIT
        ),
    )(iterate)
    return pl.pallas_call(
        last_product,
        grid=(n // 768,),
        out_shape=jax.ShapeDtypeStruct((m, n), f32),
        in_specs=[
            pl.BlockSpec((m, 768), lambda i: (0, i)),
            pl.BlockSpec((m, m), lambda i: (0, 0)),
            pl.BlockSpec((m, 768), lambda i: (0, i)),
        ],
        out_specs=pl.BlockSpec((m, 768), lambda i: (0, i)),
        compiler_params=pltpu.CompilerParams(vmem_limit_bytes=VMEM_LIMIT),
    )(partial, poly, far)


def solution(mesh):
    rows, cols = mesh.shape["row"], mesh.shape["col"]
    placed = (P("col", "row"),)

    def local(iterate):
        m, n = iterate.shape
        fits = 40 * m * m + 6 * m * n + 15000 * m < VMEM_LIMIT
        if cols == 4 and rows == 8 and m == 128 * len(FAR_STEP) and n % 768 == 0 and fits:
            return square_of_four(rows, iterate)
        return general(iterate)

    return jax.shard_map(
        local, mesh=mesh, in_specs=placed, out_specs=P("col", "row"), check_vma=False
    )
```

```python
import functools

import jax
import jax.numpy as jnp
from jax import lax
from jax.experimental import pallas as pl
from jax.experimental.pallas import tpu as pltpu
from jax.sharding import PartitionSpec as P

N = 18432


QUINTIC_A = 3.4445
QUINTIC_B = -4.775
QUINTIC_C = 2.0315

VMEM_LIMIT = 60 * 2**20
EARLY = (0,)
LAG = (4, 5)
FAR_STEP = (9, 9, 9, 9, 9, 9, 9)
ROWS_BY_ROWS = (((1,), (1,)), ((), ()))
COLS_BY_ROWS = (((0,), (0,)), ((), ()))


def general(iterate):
    inverse = 1.0 / N
    column_slab = lax.all_gather(iterate, "col", axis=0, tiled=True)
    gram_total = lax.psum_scatter(
        lax.dot_general(column_slab, iterate, ROWS_BY_ROWS, preferred_element_type=jnp.float32),
        "row",
        scatter_dimension=0,
        tiled=True,
    )
    gram_tile = (gram_total * inverse).astype(jnp.bfloat16)
    row_panel = lax.all_gather(gram_tile, "col", axis=1, tiled=True)
    square = jnp.dot(
        row_panel,
        lax.all_gather(gram_tile, "row", axis=0, tiled=True),
        preferred_element_type=jnp.float32,
    )
    poly_tile = (QUINTIC_B * gram_tile.astype(jnp.float32) + QUINTIC_C * square).astype(
        jnp.bfloat16
    )
    product = lax.dot_general(
        lax.all_gather(poly_tile, "row", axis=0, tiled=True),
        column_slab,
        COLS_BY_ROWS,
        preferred_element_type=jnp.float32,
    )
    return QUINTIC_A * iterate.astype(jnp.float32) + product


def polynomial_kernel(
    depth, inverse, early, x_in, partial_out, poly_out, far_out, pieces,
    x_ref, slab, part, paired, outgoing, incoming, own, staging, gram, poly, tile,
    x_sem, x_send, x_recv, far_send, far_recv, pair_send, pair_recv, sum_send, sum_recv,
    own_sem, along_send, along_recv, plane_send, plane_recv, relay_send, relay_recv,
    third_send, third_recv,
    stage_sem, poly_send, poly_recv, out_sem,
):
    m, n = x_ref.shape
    b = 32 * depth
    phases = m // b
    c, r = lax.axis_index("col"), lax.axis_index("row")
    z, core = r // 2, r % 2
    side = r + 1 - 2 * core
    across = {1: c + 1 - 2 * (c % 2), 2: (c + 2) % 4, 3: 3 - c}

    def there(d):
        return (z + d) % depth

    def origin(d):
        return (z + depth - d) % depth

    def remote(source, target, send, recv, row=r, col=c):
        return pltpu.make_async_remote_copy(
            src_ref=source, dst_ref=target, send_sem=send, recv_sem=recv,
            device_id={"row": row, "col": col}, device_id_type=pl.DeviceIdType.MESH,
        )

    barrier = pltpu.get_barrier_semaphore()
    partners = [(r, across[l]) for l in (1, 2, 3)] + [(side, c)]
    partners += [(2 * there(d) + core, c) for d in range(1, depth)]
    for row, col in partners:
        pl.semaphore_signal(
            barrier, inc=1, device_id={"row": row, "col": col},
            device_id_type=pl.DeviceIdType.MESH,
        )
    pl.semaphore_wait(barrier, len(partners))

    def x_copy(q, l):
        rows = pl.ds(q * b, b)
        return remote(
            x_in.at[rows], slab.at[l - 1, rows],
            x_send.at[q, l - 1], x_recv.at[q, l - 1], col=across[l],
        )

    def far_copy(q, l):
        rows = pl.ds(q * b + (l - 1) * (b // 2), b // 2)
        return remote(
            slab.at[l - 1, rows], far_out.at[rows],
            far_send.at[q, l - 1], far_recv.at[q, l - 1], col=across[3 - l],
        )

    def pair_copy(q):
        return remote(
            part.at[q % 2, 1 - core], paired.at[q], pair_send.at[q], pair_recv.at[q], row=side
        )

    def products(q):
        low, high = q * b, m - b - q * b

        def put(t, start, left, right):
            width = right.shape[0]
            total = inverse * lax.dot_general(
                left, right, ROWS_BY_ROWS, preferred_element_type=jnp.float32
            )
            total = total.reshape(depth, 2, 16, width)
            for k in (0, 1):
                part[q % 2, k, :, t, :, start : start + width] = total[:, k]

        put(0, 0, slab[0, low : low + b], x_ref[low:])
        put(0, m - low, slab[0, low : low + b], slab[1, : low + b])
        put(1, 0, slab[1, low : low + b], x_ref[low:])
        put(1, m - low, x_ref[high : high + b], x_ref[high:])
        pair_copy(q).start()

    def sum_copy(q, d):
        return remote(
            outgoing.at[q, there(d)], incoming.at[q, d - 1],
            sum_send.at[q, d - 1], sum_recv.at[q, d - 1], row=2 * there(d) + core,
        )

    def send_sums(q):
        pair_copy(q).wait_recv()
        total = part[q % 2, core] + paired[q]
        paired[q] = total
        outgoing[q] = total.astype(jnp.bfloat16)
        for d in range(1, depth):
            sum_copy(q, d).start()

    def along_copy(q, d, arriving=False):
        at = origin(d) if arriving else z
        held = pieces.at[q, :, :, at, core] if q in early else pieces.at[q, 0, :, at, core]
        return remote(
            held if q in early else own.at[q], held,
            along_send.at[q, d - 1], along_recv.at[q, d - 1], row=2 * there(d) + core,
        )

    def plane_copy(q, l):
        if q in early:
            source, held = own.at[q], pieces.at[q, l, :, z, core]
        else:
            source, held = pieces.at[q, 0, :, :, core], pieces.at[q, l, :, :, core]
        return remote(
            source, held, plane_send.at[q, l - 1], plane_recv.at[q, l - 1], col=across[l]
        )

    def relay_copy(q, l):
        if q in early:
            source, held = pieces.at[q, l, l - 1, z, core], pieces.at[q, 3, l - 1, z, core]
        else:
            source, held = pieces.at[q, l, l - 1, :, core], pieces.at[q, 3, l - 1, :, core]
        return remote(
            source, held, relay_send.at[q, l - 1], relay_recv.at[q, l - 1], col=across[3 - l]
        )

    def third_copy(q, arriving=False):
        held = pieces.at[q, :, :, :, 1 - core if arriving else core]
        return remote(held, held, third_send.at[q], third_recv.at[q], row=side)

    def own_copy(q):
        return pltpu.make_async_copy(own.at[q], pieces.at[q, 0, :, z, core], own_sem.at[q])

    def finish(q):
        total = paired[q, z]
        for d in range(1, depth):
            sum_copy(q, d).wait_recv()
            total += incoming[q, d - 1].astype(jnp.float32)
        own[q] = total.astype(jnp.bfloat16)
        own_copy(q).start()

    def start_along(q):
        for d in range(1, depth):
            along_copy(q, d).start()

    def along_arrived(q):
        for d in range(1, depth):
            along_copy(q, d, True).wait_recv()

    def start_plane(q):
        for l in (1, 2):
            plane_copy(q, l).start()

    def start_relay(q):
        for l in (1, 2):
            plane_copy(q, l).wait_recv()
        for l in (1, 2):
            relay_copy(q, l).start()

    def relay_arrived(q):
        for l in (1, 2):
            relay_copy(q, l).wait_recv()

    def first(q):
        finish(q)
        if q in early:
            start_plane(q)
        else:
            start_along(q)

    def second(q):
        own_copy(q).wait()
        if q in early:
            start_relay(q)
        else:
            along_arrived(q)
            start_plane(q)

    def third(q):
        if q in early:
            relay_arrived(q)
            start_along(q)
        else:
            start_relay(q)

    def fourth(q):
        if q in early:
            along_arrived(q)
        else:
            relay_arrived(q)
        third_copy(q).start()

    def stage(q):
        return pltpu.make_async_copy(pieces.at[q], staging.at[q % 2], stage_sem.at[q])

    def arrived(q):
        third_copy(q, True).wait_recv()
        stage(q).start()

    def assemble(q):
        stage(q).wait()
        low, high = q * b, m - b - q * b

        def place(block, row, lane_block, lane, value, flipped):
            width = value.shape[1]
            rows, lanes = block * m + row, lane_block * m + lane
            gram[rows : rows + b, lanes : lanes + width] = value
            gram[lanes : lanes + width, rows : rows + b] = flipped

        for l in range(4):
            value = staging[q % 2, l, 0].reshape(b, m + b)
            flipped = value.T
            cut = m - low
            place(l ^ 1, low, l, low, value[:, :cut], flipped[:cut])
            place(l ^ 1, low, l ^ 2, 0, value[:, cut:], flipped[cut:])
            value = staging[q % 2, l, 1].reshape(b, m + b)
            flipped = value.T
            place(l ^ 2, low, l, low, value[:, :cut], flipped[:cut])
            place(l, high, l, high, value[:, cut:], flipped[cut:])

    for q in range(2):
        for l in (1, 2):
            x_copy(q, l).start()
    pltpu.make_async_copy(x_in, x_ref, x_sem.at[0]).start()
    pltpu.make_async_copy(x_in, x_ref, x_sem.at[0]).wait()
    stages = (
        (first, (1, 1)), (second, (2, 2)), (third, (3, 3)), (fourth, LAG), (arrived, (LAG[0] + 1, LAG[1] + 1))
    )
    for step in range(phases + max(LAG) + 1):
        if step < phases:
            for l in (1, 2):
                x_copy(step, l).wait()
            if step + 2 < phases:
                for l in (1, 2):
                    x_copy(step + 2, l).start()
            if step > 1:
                pair_copy(step - 2).wait_send()
            products(step)
        for place in (0, 1, 2, 3, 4) if step < phases else (2, 1, 0, 3, 4):
            act, lags = stages[place]
            for q in range(phases):
                if q + lags[q in early] == step:
                    act(q)
            if act is first and step < phases:
                send_sums(step)
            if act is third:
                for q in range(phases):
                    if FAR_STEP[q] == step:
                        for l in (1, 2):
                            far_copy(q, l).start()
        for q in range(phases):
            if q + LAG[q in early] + 1 == step:
                assemble(q)

    width = 256
    tiles = 2 * m // width

    def poly_copy(i, half):
        lanes = pl.ds(pl.multiple_of(half * 2 * m + i * width, width), width)
        return remote(poly.at[:, lanes], poly.at[:, lanes], poly_send.at[i], poly_recv.at[i], row=side)

    def square(i, carry):
        lanes = pl.ds(pl.multiple_of(core * 2 * m + i * width, width), width)
        total = jnp.dot(gram[:m], gram[:, lanes], preferred_element_type=jnp.float32)
        kept = gram[:m, lanes].astype(jnp.float32)
        poly[:, lanes] = (QUINTIC_B * kept + QUINTIC_C * total).astype(jnp.bfloat16)
        poly_copy(i, core).start()
        return carry

    lax.fori_loop(0, tiles, square, 0)
    for i in range(tiles):
        poly_copy(i, 1 - core).wait_recv()
    keep = pltpu.make_async_copy(poly.at[:, pl.ds(3 * m, m)], poly_out, out_sem.at[2])
    keep.start()

    def out_copy(i):
        lanes = pl.ds(pl.multiple_of(i * width, width), width)
        return pltpu.make_async_copy(tile.at[i % 2], partial_out.at[:, lanes], out_sem.at[i % 2])

    def product(i, carry):
        lanes = pl.ds(pl.multiple_of(i * width, width), width)
        pl.when(i > 1)(lambda: out_copy(i - 2).wait())
        total = QUINTIC_A * x_ref[:, lanes].astype(jnp.float32)
        total += jnp.dot(poly[:, :m], x_ref[:, lanes], preferred_element_type=jnp.float32)
        for l in (1, 2):
            total += jnp.dot(
                poly[:, l * m : (l + 1) * m], slab[l - 1, :, lanes],
                preferred_element_type=jnp.float32,
            )
        tile[i % 2] = total
        out_copy(i).start()
        return carry

    lax.fori_loop(0, n // width, product, 0)
    for i in (n // width - 2, n // width - 1):
        out_copy(i).wait()
    keep.wait()
    for q in range(phases):
        for l in (1, 2):
            far_copy(q, l).wait()
    for i in range(tiles):
        poly_copy(i, core).wait_send()
    for q in range(phases):
        if q > phases - 3:
            pair_copy(q).wait_send()
        for d in range(1, depth):
            sum_copy(q, d).wait_send()
        for d in range(1, depth):
            along_copy(q, d).wait_send()
        for l in (1, 2):
            plane_copy(q, l).wait_send()
            relay_copy(q, l).wait_send()
        third_copy(q).wait_send()


def last_product(partial_ref, poly_ref, far_ref, out_ref):
    out_ref[...] = partial_ref[...] + jnp.dot(
        poly_ref[...], far_ref[...], preferred_element_type=jnp.float32
    )


def square_of_four(rows, iterate):
    m, n = iterate.shape
    depth = rows // 2
    b = 16 * rows
    phases, lanes = m // b, m + b
    bf16, f32, dma = jnp.bfloat16, jnp.float32, pltpu.SemaphoreType.DMA
    anywhere = pl.BlockSpec(memory_space=pl.ANY)
    partial, poly, far, _ = pl.pallas_call(
        functools.partial(polynomial_kernel, depth, 1.0 / N, EARLY),
        out_shape=(
            jax.ShapeDtypeStruct((m, n), f32),
            jax.ShapeDtypeStruct((m, m), bf16),
            jax.ShapeDtypeStruct((m, n), bf16),
            jax.ShapeDtypeStruct((phases, 4, 2, depth, 2, 16, lanes), bf16),
        ),
        in_specs=[anywhere],
        out_specs=(anywhere,) * 4,
        scratch_shapes=[
            pltpu.VMEM((m, n), bf16),
            pltpu.VMEM((2, m, n), bf16),
            pltpu.VMEM((2, 2, depth, 2, 16, lanes), f32),
            pltpu.VMEM((phases, depth, 2, 16, lanes), f32),
            pltpu.VMEM((phases, depth, 2, 16, lanes), bf16),
            pltpu.VMEM((phases, depth - 1, 2, 16, lanes), bf16),
            pltpu.VMEM((phases, 2, 16, lanes), bf16),
            pltpu.VMEM((2, 4, 2, depth, 2, 16, lanes), bf16),
            pltpu.VMEM((4 * m, 4 * m), bf16),
            pltpu.VMEM((m, 4 * m), bf16),
            pltpu.VMEM((2, m, 256), f32),
            dma((1,)),
            dma((phases, 2)), dma((phases, 2)),
            dma((phases, 2)), dma((phases, 2)),
            dma((phases,)), dma((phases,)),
            dma((phases, depth - 1)), dma((phases, depth - 1)),
            dma((phases,)),
            dma((phases, depth - 1)), dma((phases, depth - 1)),
            dma((phases, 2)), dma((phases, 2)),
            dma((phases, 2)), dma((phases, 2)),
            dma((phases,)), dma((phases,)),
            dma((phases,)),
            dma((2 * m // 256,)), dma((2 * m // 256,)),
            dma((3,)),
        ],
        compiler_params=pltpu.CompilerParams(
            collective_id=0, has_side_effects=True, vmem_limit_bytes=VMEM_LIMIT
        ),
    )(iterate)
    return pl.pallas_call(
        last_product,
        grid=(n // 768,),
        out_shape=jax.ShapeDtypeStruct((m, n), f32),
        in_specs=[
            pl.BlockSpec((m, 768), lambda i: (0, i)),
            pl.BlockSpec((m, m), lambda i: (0, 0)),
            pl.BlockSpec((m, 768), lambda i: (0, i)),
        ],
        out_specs=pl.BlockSpec((m, 768), lambda i: (0, i)),
        compiler_params=pltpu.CompilerParams(vmem_limit_bytes=VMEM_LIMIT),
    )(partial, poly, far)


def solution(mesh):
    rows, cols = mesh.shape["row"], mesh.shape["col"]
    placed = (P("col", "row"),)

    def local(iterate):
        m, n = iterate.shape
        fits = 40 * m * m + 6 * m * n + 15000 * m < VMEM_LIMIT
        if cols == 4 and rows == 8 and m == 128 * len(FAR_STEP) and n % 768 == 0 and fits:
            return square_of_four(rows, iterate)
        return general(iterate)

    return jax.shard_map(
        local, mesh=mesh, in_specs=placed, out_specs=P("col", "row"), check_vma=False
    )
```

```python
import functools

import jax
import jax.numpy as jnp
from jax import lax
from jax.experimental import pallas as pl
from jax.experimental.pallas import tpu as pltpu
from jax.sharding import PartitionSpec as P

N = 18432


QUINTIC_A = 3.4445
QUINTIC_B = -4.775
QUINTIC_C = 2.0315

VMEM_LIMIT = 60 * 2**20
EARLY = (0,)
LAG = (4, 5)
FAR_STEP = (9, 9, 9, 9, 9, 9, 9)
ROWS_BY_ROWS = (((1,), (1,)), ((), ()))
COLS_BY_ROWS = (((0,), (0,)), ((), ()))


def general(iterate):
    inverse = 1.0 / N
    column_slab = lax.all_gather(iterate, "col", axis=0, tiled=True)
    gram_total = lax.psum_scatter(
        lax.dot_general(column_slab, iterate, ROWS_BY_ROWS, preferred_element_type=jnp.float32),
        "row",
        scatter_dimension=0,
        tiled=True,
    )
    gram_tile = (gram_total * inverse).astype(jnp.bfloat16)
    row_panel = lax.all_gather(gram_tile, "col", axis=1, tiled=True)
    square = jnp.dot(
        row_panel,
        lax.all_gather(gram_tile, "row", axis=0, tiled=True),
        preferred_element_type=jnp.float32,
    )
    poly_tile = (QUINTIC_B * gram_tile.astype(jnp.float32) + QUINTIC_C * square).astype(
        jnp.bfloat16
    )
    product = lax.dot_general(
        lax.all_gather(poly_tile, "row", axis=0, tiled=True),
        column_slab,
        COLS_BY_ROWS,
        preferred_element_type=jnp.float32,
    )
    return QUINTIC_A * iterate.astype(jnp.float32) + product


def polynomial_kernel(
    depth, inverse, early, x_in, partial_out, poly_out, far_out, pieces,
    x_ref, slab, part, paired, outgoing, incoming, own, staging, gram, poly, tile,
    x_sem, x_send, x_recv, far_send, far_recv, pair_send, pair_recv, sum_send, sum_recv,
    own_sem, along_send, along_recv, plane_send, plane_recv, relay_send, relay_recv,
    third_send, third_recv,
    stage_sem, poly_send, poly_recv, out_sem,
):
    m, n = x_ref.shape
    b = 32 * depth
    phases = m // b
    c, r = lax.axis_index("col"), lax.axis_index("row")
    z, core = r // 2, r % 2
    side = r + 1 - 2 * core
    across = {1: c + 1 - 2 * (c % 2), 2: (c + 2) % 4, 3: 3 - c}

    def there(d):
        return (z + d) % depth

    def origin(d):
        return (z + depth - d) % depth

    def remote(source, target, send, recv, row=r, col=c):
        return pltpu.make_async_remote_copy(
            src_ref=source, dst_ref=target, send_sem=send, recv_sem=recv,
            device_id={"row": row, "col": col}, device_id_type=pl.DeviceIdType.MESH,
        )

    barrier = pltpu.get_barrier_semaphore()
    partners = [(r, across[l]) for l in (1, 2, 3)] + [(side, c)]
    partners += [(2 * there(d) + core, c) for d in range(1, depth)]
    for row, col in partners:
        pl.semaphore_signal(
            barrier, inc=1, device_id={"row": row, "col": col},
            device_id_type=pl.DeviceIdType.MESH,
        )
    pl.semaphore_wait(barrier, len(partners))

    def x_copy(q, l):
        rows = pl.ds(q * b, b)
        return remote(
            x_in.at[rows], slab.at[l - 1, rows],
            x_send.at[q, l - 1], x_recv.at[q, l - 1], col=across[l],
        )

    def far_copy(q, l):
        rows = pl.ds(q * b + (l - 1) * (b // 2), b // 2)
        return remote(
            slab.at[l - 1, rows], far_out.at[rows],
            far_send.at[q, l - 1], far_recv.at[q, l - 1], col=across[3 - l],
        )

    def pair_copy(q):
        return remote(
            part.at[q % 2, 1 - core], paired.at[q], pair_send.at[q], pair_recv.at[q], row=side
        )

    def products(q):
        low, high = q * b, m - b - q * b

        def put(t, start, left, right):
            width = right.shape[0]
            total = inverse * lax.dot_general(
                left, right, ROWS_BY_ROWS, preferred_element_type=jnp.float32
            )
            total = total.reshape(depth, 2, 16, width)
            for k in (0, 1):
                part[q % 2, k, :, t, :, start : start + width] = total[:, k]

        put(0, 0, slab[0, low : low + b], x_ref[low:])
        put(0, m - low, slab[0, low : low + b], slab[1, : low + b])
        put(1, 0, slab[1, low : low + b], x_ref[low:])
        put(1, m - low, x_ref[high : high + b], x_ref[high:])
        pair_copy(q).start()

    def sum_copy(q, d):
        return remote(
            outgoing.at[q, there(d)], incoming.at[q, d - 1],
            sum_send.at[q, d - 1], sum_recv.at[q, d - 1], row=2 * there(d) + core,
        )

    def send_sums(q):
        pair_copy(q).wait_recv()
        total = part[q % 2, core] + paired[q]
        paired[q] = total
        outgoing[q] = total.astype(jnp.bfloat16)
        for d in range(1, depth):
            sum_copy(q, d).start()

    def along_copy(q, d, arriving=False):
        at = origin(d) if arriving else z
        held = pieces.at[q, :, :, at, core] if q in early else pieces.at[q, 0, :, at, core]
        return remote(
            held if q in early else own.at[q], held,
            along_send.at[q, d - 1], along_recv.at[q, d - 1], row=2 * there(d) + core,
        )

    def plane_copy(q, l):
        if q in early:
            source, held = own.at[q], pieces.at[q, l, :, z, core]
        else:
            source, held = pieces.at[q, 0, :, :, core], pieces.at[q, l, :, :, core]
        return remote(
            source, held, plane_send.at[q, l - 1], plane_recv.at[q, l - 1], col=across[l]
        )

    def relay_copy(q, l):
        if q in early:
            source, held = pieces.at[q, l, l - 1, z, core], pieces.at[q, 3, l - 1, z, core]
        else:
            source, held = pieces.at[q, l, l - 1, :, core], pieces.at[q, 3, l - 1, :, core]
        return remote(
            source, held, relay_send.at[q, l - 1], relay_recv.at[q, l - 1], col=across[3 - l]
        )

    def third_copy(q, arriving=False):
        held = pieces.at[q, :, :, :, 1 - core if arriving else core]
        return remote(held, held, third_send.at[q], third_recv.at[q], row=side)

    def own_copy(q):
        return pltpu.make_async_copy(own.at[q], pieces.at[q, 0, :, z, core], own_sem.at[q])

    def finish(q):
        total = paired[q, z]
        for d in range(1, depth):
            sum_copy(q, d).wait_recv()
            total += incoming[q, d - 1].astype(jnp.float32)
        own[q] = total.astype(jnp.bfloat16)
        own_copy(q).start()

    def start_along(q):
        for d in range(1, depth):
            along_copy(q, d).start()

    def along_arrived(q):
        for d in range(1, depth):
            along_copy(q, d, True).wait_recv()

    def start_plane(q):
        for l in (1, 2):
            plane_copy(q, l).start()

    def start_relay(q):
        for l in (1, 2):
            plane_copy(q, l).wait_recv()
        for l in (1, 2):
            relay_copy(q, l).start()

    def relay_arrived(q):
        for l in (1, 2):
            relay_copy(q, l).wait_recv()

    def first(q):
        finish(q)
        if q in early:
            start_plane(q)
        else:
            start_along(q)

    def second(q):
        own_copy(q).wait()
        if q in early:
            start_relay(q)
        else:
            along_arrived(q)
            start_plane(q)

    def third(q):
        if q in early:
            relay_arrived(q)
            start_along(q)
        else:
            start_relay(q)

    def fourth(q):
        if q in early:
            along_arrived(q)
        else:
            relay_arrived(q)
        third_copy(q).start()

    def stage(q):
        return pltpu.make_async_copy(pieces.at[q], staging.at[q % 2], stage_sem.at[q])

    def arrived(q):
        third_copy(q, True).wait_recv()
        stage(q).start()

    def assemble(q):
        stage(q).wait()
        low, high = q * b, m - b - q * b

        def place(block, row, lane_block, lane, value, flipped):
            width = value.shape[1]
            rows, lanes = block * m + row, lane_block * m + lane
            gram[rows : rows + b, lanes : lanes + width] = value
            gram[lanes : lanes + width, rows : rows + b] = flipped

        for l in range(4):
            value = staging[q % 2, l, 0].reshape(b, m + b)
            flipped = value.T
            cut = m - low
            place(l ^ 1, low, l, low, value[:, :cut], flipped[:cut])
            place(l ^ 1, low, l ^ 2, 0, value[:, cut:], flipped[cut:])
            value = staging[q % 2, l, 1].reshape(b, m + b)
            flipped = value.T
            place(l ^ 2, low, l, low, value[:, :cut], flipped[:cut])
            place(l, high, l, high, value[:, cut:], flipped[cut:])

    for q in range(3):
        for l in (1, 2):
            x_copy(q, l).start()
    pltpu.make_async_copy(x_in, x_ref, x_sem.at[0]).start()
    pltpu.make_async_copy(x_in, x_ref, x_sem.at[0]).wait()
    stages = (
        (first, (1, 1)), (second, (2, 2)), (third, (3, 3)), (fourth, LAG), (arrived, (LAG[0] + 1, LAG[1] + 1))
    )
    for step in range(phases + max(LAG) + 1):
        if step < phases:
            for l in (1, 2):
                x_copy(step, l).wait()
            if step + 3 < phases:
                for l in (1, 2):
                    x_copy(step + 3, l).start()
            if step > 1:
                pair_copy(step - 2).wait_send()
            products(step)
        for place in (0, 1, 2, 3, 4) if step < phases else (2, 1, 0, 3, 4):
            act, lags = stages[place]
            for q in range(phases):
                if q + lags[q in early] == step:
                    act(q)
            if act is first and step < phases:
                send_sums(step)
            if act is third:
                for q in range(phases):
                    if FAR_STEP[q] == step:
                        for l in (1, 2):
                            far_copy(q, l).start()
        for q in range(phases):
            if q + LAG[q in early] + 1 == step:
                assemble(q)

    width = 256
    tiles = 2 * m // width

    def poly_copy(i, half):
        lanes = pl.ds(pl.multiple_of(half * 2 * m + i * width, width), width)
        return remote(poly.at[:, lanes], poly.at[:, lanes], poly_send.at[i], poly_recv.at[i], row=side)

    def square(i, carry):
        lanes = pl.ds(pl.multiple_of(core * 2 * m + i * width, width), width)
        total = jnp.dot(gram[:m], gram[:, lanes], preferred_element_type=jnp.float32)
        kept = gram[:m, lanes].astype(jnp.float32)
        poly[:, lanes] = (QUINTIC_B * kept + QUINTIC_C * total).astype(jnp.bfloat16)
        poly_copy(i, core).start()
        return carry

    lax.fori_loop(0, tiles, square, 0)
    for i in range(tiles):
        poly_copy(i, 1 - core).wait_recv()
    keep = pltpu.make_async_copy(poly.at[:, pl.ds(3 * m, m)], poly_out, out_sem.at[2])
    keep.start()

    def out_copy(i):
        lanes = pl.ds(pl.multiple_of(i * width, width), width)
        return pltpu.make_async_copy(tile.at[i % 2], partial_out.at[:, lanes], out_sem.at[i % 2])

    def product(i, carry):
        lanes = pl.ds(pl.multiple_of(i * width, width), width)
        pl.when(i > 1)(lambda: out_copy(i - 2).wait())
        total = QUINTIC_A * x_ref[:, lanes].astype(jnp.float32)
        total += jnp.dot(poly[:, :m], x_ref[:, lanes], preferred_element_type=jnp.float32)
        for l in (1, 2):
            total += jnp.dot(
                poly[:, l * m : (l + 1) * m], slab[l - 1, :, lanes],
                preferred_element_type=jnp.float32,
            )
        tile[i % 2] = total
        out_copy(i).start()
        return carry

    lax.fori_loop(0, n // width, product, 0)
    for i in (n // width - 2, n // width - 1):
        out_copy(i).wait()
    keep.wait()
    for q in range(phases):
        for l in (1, 2):
            far_copy(q, l).wait()
    for i in range(tiles):
        poly_copy(i, core).wait_send()
    for q in range(phases):
        if q > phases - 3:
            pair_copy(q).wait_send()
        for d in range(1, depth):
            sum_copy(q, d).wait_send()
        for d in range(1, depth):
            along_copy(q, d).wait_send()
        for l in (1, 2):
            plane_copy(q, l).wait_send()
            relay_copy(q, l).wait_send()
        third_copy(q).wait_send()


def last_product(partial_ref, poly_ref, far_ref, out_ref):
    out_ref[...] = partial_ref[...] + jnp.dot(
        poly_ref[...], far_ref[...], preferred_element_type=jnp.float32
    )


def square_of_four(rows, iterate):
    m, n = iterate.shape
    depth = rows // 2
    b = 16 * rows
    phases, lanes = m // b, m + b
    bf16, f32, dma = jnp.bfloat16, jnp.float32, pltpu.SemaphoreType.DMA
    anywhere = pl.BlockSpec(memory_space=pl.ANY)
    partial, poly, far, _ = pl.pallas_call(
        functools.partial(polynomial_kernel, depth, 1.0 / N, EARLY),
        out_shape=(
            jax.ShapeDtypeStruct((m, n), f32),
            jax.ShapeDtypeStruct((m, m), bf16),
            jax.ShapeDtypeStruct((m, n), bf16),
            jax.ShapeDtypeStruct((phases, 4, 2, depth, 2, 16, lanes), bf16),
        ),
        in_specs=[anywhere],
        out_specs=(anywhere,) * 4,
        scratch_shapes=[
            pltpu.VMEM((m, n), bf16),
            pltpu.VMEM((2, m, n), bf16),
            pltpu.VMEM((2, 2, depth, 2, 16, lanes), f32),
            pltpu.VMEM((phases, depth, 2, 16, lanes), f32),
            pltpu.VMEM((phases, depth, 2, 16, lanes), bf16),
            pltpu.VMEM((phases, depth - 1, 2, 16, lanes), bf16),
            pltpu.VMEM((phases, 2, 16, lanes), bf16),
            pltpu.VMEM((2, 4, 2, depth, 2, 16, lanes), bf16),
            pltpu.VMEM((4 * m, 4 * m), bf16),
            pltpu.VMEM((m, 4 * m), bf16),
            pltpu.VMEM((2, m, 256), f32),
            dma((1,)),
            dma((phases, 2)), dma((phases, 2)),
            dma((phases, 2)), dma((phases, 2)),
            dma((phases,)), dma((phases,)),
            dma((phases, depth - 1)), dma((phases, depth - 1)),
            dma((phases,)),
            dma((phases, depth - 1)), dma((phases, depth - 1)),
            dma((phases, 2)), dma((phases, 2)),
            dma((phases, 2)), dma((phases, 2)),
            dma((phases,)), dma((phases,)),
            dma((phases,)),
            dma((2 * m // 256,)), dma((2 * m // 256,)),
            dma((3,)),
        ],
        compiler_params=pltpu.CompilerParams(
            collective_id=0, has_side_effects=True, vmem_limit_bytes=VMEM_LIMIT
        ),
    )(iterate)
    return pl.pallas_call(
        last_product,
        grid=(n // 768,),
        out_shape=jax.ShapeDtypeStruct((m, n), f32),
        in_specs=[
            pl.BlockSpec((m, 768), lambda i: (0, i)),
            pl.BlockSpec((m, m), lambda i: (0, 0)),
            pl.BlockSpec((m, 768), lambda i: (0, i)),
        ],
        out_specs=pl.BlockSpec((m, 768), lambda i: (0, i)),
        compiler_params=pltpu.CompilerParams(vmem_limit_bytes=VMEM_LIMIT),
    )(partial, poly, far)


def solution(mesh):
    rows, cols = mesh.shape["row"], mesh.shape["col"]
    placed = (P("col", "row"),)

    def local(iterate):
        m, n = iterate.shape
        fits = 40 * m * m + 6 * m * n + 15000 * m < VMEM_LIMIT
        if cols == 4 and rows == 8 and m == 128 * len(FAR_STEP) and n % 768 == 0 and fits:
            return square_of_four(rows, iterate)
        return general(iterate)

    return jax.shard_map(
        local, mesh=mesh, in_specs=placed, out_specs=P("col", "row"), check_vma=False
    )
```
